256 devices in a mesh: req: 64 (over y, z, core), tp: 4 (over x).
Axes of the slice: x: 4, y: 4, z: 8, core: 2. Of those that a mesh axis runs over, the one named last changes fastest.
Arguments:
- patches: bfloat16 [16384, 1280], P('req'), may hold values from -6 to 6
- half_grid: int32 [64, 2], P('req'), may hold values from 6 to 8
- text_embed: bfloat16 [12288, 1280], P('req'), may hold values from -6 to 6
- dest_dev: int32 [4096], P('req'), may hold values from 0 to 63, as said below
- dest_pos: int32 [4096], P('req'), may hold values from 0 to 191, as said below
- text_len: int32 [64], P('req'), may hold values from 1 to 128, as said below
- enc_qkv: bfloat16 [1280, 3840], P('req', 'tp')
- enc_out_t: bfloat16 [1280, 1280], P('req', 'tp'), may hold values from -0.15625 to 0.15625
- enc_up: bfloat16 [1280, 5120], P('req', 'tp'), may hold values from -0.15625 to 0.15625
- enc_down_t: bfloat16 [1280, 5120], P('req', 'tp'), may hold values from -0.078125 to 0.078125
- merge_t: bfloat16 [1280, 5120], P('req', 'tp'), may hold values from -0.078125 to 0.078125
- dec_qkv: bfloat16 [1280, 3840], P('req', 'tp')
- dec_out_t: bfloat16 [1280, 1280], P('req', 'tp'), may hold values from -0.15625 to 0.15625
- dec_up: bfloat16 [1280, 5120], P('req', 'tp'), may hold values from -0.15625 to 0.15625
- dec_down_t: bfloat16 [1280, 5120], P('req', 'tp'), may hold values from -0.078125 to 0.078125
Outputs:
- decoded: bfloat16 [12288, 1280], P('req')
The draws below stay inside these ranges and needn't reach their ends.
Inputs may be any that keep to these rules, and one draw needn't show every extreme that they name: `dest_dev`: the slots of one device go in runs to destination devices; at most 2 slots of one device name one destination device, exactly 2 for some pairs; every device is named by exactly 64 slots in all. `dest_pos`: positions named for one destination device are distinct and below 64 plus its text_len. `text_len`: some request has exactly 128.
All inputs are finite; a program needn't handle non-finite values.
Results may differ from the reference program's by a relative error of at most 0.024.
Values may be sent and summed in bfloat16 or wider, within the bound.
A program may use at most 64 MiB of HBM per device.

```python
import jax
import jax.numpy as jnp
from jax import lax

D = 1280
HEADS = 16
HEAD_DIM = 80
FF = 5120
GRID = 16
TXT = 128
M_IMG = 64
M_DEV = 64
SEQ = 192
REQS = 64
IMAGES = 64
ENC_TOTAL = 16384
MERGED = 4096
DEC_TOTAL = 12288


def qkv_table(key):
    base_table = jax.random.normal(jax.random.fold_in(key, 101), (D, HEADS, 3, HEAD_DIM), jnp.float32) * D ** (-0.5)
    return base_table.reshape(D, HEADS * 3 * HEAD_DIM)


def draw_enc_qkv(key, part):
    return qkv_table(jax.random.fold_in(key, 1)).astype(jnp.bfloat16)


def draw_dec_qkv(key, part):
    return qkv_table(jax.random.fold_in(key, 2)).astype(jnp.bfloat16)


def permute_row(row_key):
    return jax.random.permutation(row_key, SEQ).astype(jnp.int32)


def route_table(key):
    senders = REQS
    slot_count = M_DEV
    even_share = slot_count // senders
    spread_step = max(even_share // 2, 1)
    group_size = senders // 4
    shuffle_order = jax.random.permutation(jax.random.fold_in(key, 201), senders)
    pattern = jnp.full((senders,), even_share, jnp.int32)
    pattern = pattern.at[shuffle_order[:group_size]].add(spread_step)
    pattern = pattern.at[shuffle_order[group_size:2 * group_size]].add(-spread_step)
    run_ends = jnp.cumsum(pattern).astype(jnp.int32)
    run_starts = run_ends - pattern
    slot_ids = jnp.arange(slot_count, dtype=jnp.int32)
    offset = jnp.sum((run_ends[None, :] <= slot_ids[:, None]).astype(jnp.int32), axis=1)
    within = slot_ids - run_starts[offset]
    sender_index = jnp.arange(senders, dtype=jnp.int32)
    target = (sender_index[:, None] + offset[None, :]) % senders
    incoming = pattern[(sender_index[:, None] - sender_index[None, :]) % senders]
    before = jnp.cumsum(incoming, axis=1).astype(jnp.int32) - incoming
    slot_rank = before[target, sender_index[:, None]] + within[None, :]
    text_limit = jax.random.randint(jax.random.fold_in(key, 202), (senders,), 1, TXT + 1)
    fullest = jax.random.randint(jax.random.fold_in(key, 203), (), 0, senders)
    text_limit = jnp.where(sender_index == fullest, TXT, text_limit).astype(jnp.int32)
    length = slot_count + text_limit
    row_keys = jax.random.split(jax.random.fold_in(key, 204), senders)
    shuffled = jax.vmap(permute_row)(row_keys)
    seq_index = jnp.arange(SEQ, dtype=jnp.int32)
    ranking = shuffled + jnp.where(seq_index[None, :] < length[:, None], 0, SEQ).astype(jnp.int32)
    chosen = jnp.sort(jnp.argsort(ranking, axis=1, stable=True)[:, :slot_count].astype(jnp.int32), axis=1)
    position = chosen[target, slot_rank]
    return (target.reshape(-1).astype(jnp.int32), position.reshape(-1).astype(jnp.int32), text_limit)


def draw_dest_dev(key, part):
    return route_table(key)[0]


def draw_dest_pos(key, part):
    return route_table(key)[1]


def draw_text_len(key, part):
    return route_table(key)[2]


def set_ends(entries, stream_key, smallest, top_value):
    longest = entries.shape.index(max(entries.shape))
    spots = []
    for shift in (0, 1):
        where = [jax.random.randint(jax.random.fold_in(stream_key, axis), (), 0, length) for axis, length in enumerate(entries.shape)]
        where[longest] = (where[longest] + shift) % entries.shape[longest]
        spots.append(tuple(where))
    return entries.at[spots[0]].set(smallest).at[spots[1]].set(top_value)


def block_levels(key, extent, cuts, least, high):
    def one(axis_at, shards_of):
        draws = jax.random.uniform(jax.random.fold_in(jax.random.fold_in(key, 6), axis_at), (shards_of,), jnp.float32, least / len(cuts), high / len(cuts))
        return jnp.repeat(jnp.exp(draws), extent[axis_at] // shards_of).reshape((-1,) + (1,) * (len(extent) - axis_at - 1))

    factor_of = one(*cuts[0])
    for cut in cuts[1:]:
        factor_of = factor_of * one(*cut)
    return factor_of


def bell_draw(stream_key, extent, scale, bound, shards=(), held_as=jnp.bfloat16):
    array = jax.random.normal(stream_key, extent, jnp.float32) * scale
    if len(shards) > 0:
        array = block_levels(stream_key, extent, shards, -0.22, 0.18) * array
    return jnp.clip(array, min=-bound, max=bound).astype(held_as)


def setup_inputs(seed: int = 0) -> dict:
    seeds = jax.random.split(jax.random.key(seed), 16)
    return {
        "patches": bell_draw(seeds[0], (ENC_TOTAL, D), 1.0, 6.0, ((0, 64),)),
        "half_grid": set_ends(jax.random.randint(seeds[1], (IMAGES, 2), GRID // 4 + 2, GRID // 2 + 1), jax.random.fold_in(seeds[1], 1), GRID // 4 + 2, (GRID // 2 + 1) - 1).astype(jnp.int32),
        "text_embed": bell_draw(seeds[2], (DEC_TOTAL, D), 1.0, 6.0, ((0, 64),)),
        "dest_dev": draw_dest_dev(jax.random.fold_in(seeds[15], 71), 0),
        "dest_pos": draw_dest_pos(jax.random.fold_in(seeds[15], 71), 0),
        "text_len": draw_text_len(jax.random.fold_in(seeds[15], 71), 0),
        "enc_qkv": draw_enc_qkv(jax.random.fold_in(seeds[15], 71), 0),
        "enc_out_t": bell_draw(seeds[7], (D, D), D ** -0.5, 0.15625, ((0, 64), (1, 4))),
        "enc_up": bell_draw(seeds[8], (D, FF), D ** -0.5, 0.15625, ((0, 64), (1, 4))),
        "enc_down_t": bell_draw(seeds[9], (D, FF), FF ** -0.5, 0.078125, ((0, 64), (1, 4))),
        "merge_t": bell_draw(seeds[10], (D, 4 * D), (4 * D) ** -0.5, 0.078125, ((0, 64), (1, 4))),
        "dec_qkv": draw_dec_qkv(jax.random.fold_in(seeds[15], 71), 0),
        "dec_out_t": bell_draw(seeds[12], (D, D), D ** -0.5, 0.15625, ((0, 64), (1, 4))),
        "dec_up": bell_draw(seeds[13], (D, FF), D ** -0.5, 0.15625, ((0, 64), (1, 4))),
        "dec_down_t": bell_draw(seeds[14], (D, FF), FF ** -0.5, 0.078125, ((0, 64), (1, 4))),
    }


EPS = 1e-06

def normalize(stream):
    values_f = stream.astype(jnp.float32)
    center = values_f - lax.optimization_barrier(jnp.mean(values_f, axis=-1, keepdims=True))
    spread = lax.optimization_barrier(jnp.mean(center * center, axis=-1, keepdims=True))
    return (center * lax.rsqrt(spread + EPS)).astype(jnp.bfloat16)

def attention(normed, w_qkv, w_out_t, allowed):
    length = normed.shape[0]
    projected = jnp.dot(normed, w_qkv, preferred_element_type=jnp.float32).astype(jnp.bfloat16)
    projected = projected.reshape(length, -1, 3, HEAD_DIM).astype(jnp.float32)
    queries = projected[:, :, 0]
    key_part = projected[:, :, 1]
    value_part = projected[:, :, 2]
    scores = jnp.einsum('qhd,khd->hqk', queries, key_part) * HEAD_DIM ** (-0.5)
    scores = jnp.where(allowed[None], scores, -1e+30)
    highest = lax.optimization_barrier(jnp.max(scores, axis=-1, keepdims=True))
    exponent = jnp.exp(scores - highest)
    weights_soft = (exponent / lax.optimization_barrier(jnp.sum(exponent, axis=-1, keepdims=True))).astype(jnp.bfloat16)
    heads_out = jnp.einsum('hqk,khd->qhd', weights_soft.astype(jnp.float32), value_part)
    heads_out = heads_out.astype(jnp.bfloat16).reshape(length, -1)
    return jnp.dot(heads_out, w_out_t.T, preferred_element_type=jnp.float32)

def transformer_layer(stream, weights, allowed):
    w_qkv, w_out_t, w_up, w_down_t = weights
    middle = (stream.astype(jnp.float32) + attention(normalize(stream), w_qkv, w_out_t, allowed)).astype(jnp.bfloat16)
    hidden = jax.nn.gelu(jnp.dot(normalize(middle), w_up, preferred_element_type=jnp.float32), approximate=False)
    hidden = hidden.astype(jnp.bfloat16)
    result_rows = middle.astype(jnp.float32) + jnp.dot(hidden, w_down_t.T, preferred_element_type=jnp.float32)
    return result_rows.astype(jnp.bfloat16)

def reference(patches, half_grid, text_embed, dest_dev, dest_pos, text_len, enc_qkv, enc_out_t, enc_up, enc_down_t, merge_t, dec_qkv, dec_out_t, dec_up, dec_down_t):
    per_image = GRID * GRID
    patch_index = jnp.arange(per_image, dtype=jnp.int32)
    key_valid = ((patch_index // GRID)[None, :] < 2 * half_grid[:, 0:1]) & ((patch_index % GRID)[None, :] < 2 * half_grid[:, 1:2])
    images = patches.reshape(IMAGES, per_image, D)
    enc_weights = (enc_qkv, enc_out_t, enc_up, enc_down_t)

    def run_image(bundle):
        return transformer_layer(bundle[0], enc_weights, bundle[1][None, :])
    encoded = lax.map(run_image, (images, key_valid))
    half_side = GRID // 2
    blocks = encoded.reshape(IMAGES, half_side, 2, half_side, 2, D).transpose(0, 1, 3, 2, 4, 5).reshape(MERGED, 4 * D)
    merged = jnp.dot(blocks, merge_t.T, preferred_element_type=jnp.float32).astype(jnp.bfloat16)
    cell_index = jnp.arange(M_IMG, dtype=jnp.int32)
    slot_valid = ((cell_index // half_side)[None, :] < half_grid[:, 0:1]) & ((cell_index % half_side)[None, :] < half_grid[:, 1:2])
    slot_valid = slot_valid.reshape(MERGED)
    target_pos = jnp.where(slot_valid, dest_pos, SEQ).astype(jnp.int32)
    dec_input = text_embed.reshape(REQS, SEQ, D).at[dest_dev, target_pos].set(merged, mode='drop')
    positions = jnp.arange(SEQ, dtype=jnp.int32)
    causal = positions[:, None] >= positions[None, :]
    dec_weights = (dec_qkv, dec_out_t, dec_up, dec_down_t)

    def run_request(sequence):
        return transformer_layer(sequence, dec_weights, causal)
    decoded = lax.map(run_request, dec_input)
    lengths = M_DEV + text_len
    keep_mask = positions[None, :] < lengths[:, None]
    decoded = jnp.where(keep_mask[:, :, None], decoded, jnp.zeros_like(decoded))
    return decoded.astype(jnp.bfloat16).reshape(DEC_TOTAL, D)
```

```python
import functools

import jax
import jax.numpy as jnp
from jax import lax
from jax.experimental import pallas as pl
from jax.experimental.pallas import tpu as pltpu
from jax.sharding import PartitionSpec as P

MESH = pl.DeviceIdType.MESH
NY, NZ, NX = 4, 8, 4
GROUPS = 7
D = 1280
HALF = 640
SHARD = 20
EVENTS = 11
CHIP_EVENTS = 8


class Place:
    def __init__(self):
        req = lax.axis_index("req")
        self.x = lax.axis_index("tp")
        self.c = lax.rem(req, 2)
        self.z = lax.rem(req // 2, NZ)
        self.y = req // (2 * NZ)

    def yy(self, step):
        return lax.rem(self.y + (step + NY), NY)

    def zz(self, step):
        return lax.rem(self.z + (step + NZ), NZ)

    def xx(self, step):
        return lax.rem(self.x + (step + NX), NX)

    def dev(self, y=0, z=0, flip=False):
        core = 1 - self.c if flip else self.c
        return ((self.yy(y) * NZ + self.zz(z)) * 2 + core, self.x)

    def along_x(self, step):
        return ((self.y * NZ + self.z) * 2 + self.c, self.xx(step))


def remote(src, dst, send, recv, device):
    return pltpu.make_async_remote_copy(
        src_ref=src, dst_ref=dst, send_sem=send, recv_sem=recv,
        device_id=device, device_id_type=MESH,
    )


class Gather:
    def __init__(self, place, w, own, pair, sems):
        self.p, self.w, self.own, self.pair = place, w, own, pair
        self.send, self.recv, self.csend, self.crecv, self.psend, self.precv = sems

    def pair_copy(self, part):
        p = self.p
        groups = pl.ds(0, 1) if part == 0 else pl.ds(1, GROUPS - 1)
        return remote(
            self.own.at[1 - p.c, groups], self.pair.at[groups],
            self.psend.at[part], self.precv.at[part], p.dev(flip=True),
        )

    def assemble(self, g):
        p = self.p
        mine, theirs = self.own[p.c, g], self.pair[g]
        first = p.c == 0
        top = jnp.where(first, mine, theirs)
        low = jnp.where(first, theirs, mine)
        columns = pl.ds(pl.multiple_of(p.c * HALF, 128), HALF)
        self.w[g, p.y, p.z, :, columns] = jnp.concatenate([top, low], axis=0)

    def part(self, g, core, ys, zs):
        return self.w.at[g, ys, zs, :, core * HALF:(core + 1) * HALF]

    def event(self, core, g, e):
        p = self.p
        one = lambda v: pl.ds(v, 1)
        if core == 0:
            every = pl.ds(0, NY)
            if e == 0:
                return one(p.y), one(p.z), one(p.yy(-1)), one(p.z), 1, 0
            if e == 1:
                return one(p.y), one(p.z), one(p.yy(1)), one(p.z), -1, 0
            if e == 2:
                d = 1 if g % 2 == 0 else -1
                return one(p.yy(-d)), one(p.z), one(p.yy(2)), one(p.z), d, 0
            if e in (9, 10):
                d = 1 if e == 9 else -1
                ys = pl.ds(0, 2) if e == 9 else pl.ds(2, 2)
                return ys, one(p.zz(-3 * d)), ys, one(p.zz(4)), 0, d
            hop, d = (e - 3) // 2, 1 if (e - 3) % 2 == 0 else -1
            return every, one(p.zz(-hop * d)), every, one(p.zz(-(hop + 1) * d)), 0, d
        if e < 6:
            hop, d = e // 2, 1 if e % 2 == 0 else -1
            return one(p.y), one(p.zz(-hop * d)), one(p.y), one(p.zz(-(hop + 1) * d)), 0, d
        if e == 6:
            d = 1 if g % 2 == 0 else -1
            return one(p.y), one(p.zz(-3 * d)), one(p.y), one(p.zz(4)), 0, d
        if e in (7, 8):
            d = 1 if e == 7 else -1
            return one(p.y), pl.ds(0, NZ), one(p.yy(-d)), pl.ds(0, NZ), d, 0
        d = 1 if e == 9 else -1
        zs = pl.ds(0, NZ // 2) if e == 9 else pl.ds(NZ // 2, NZ // 2)
        return one(p.yy(-d)), zs, one(p.yy(2)), zs, d, 0

    def copy(self, core, g, e, receive=False):
        sy, sz, ry, rz, dy, dz = self.event(core, g, e)
        ref = self.part(g, core, ry, rz) if receive else self.part(g, core, sy, sz)
        return remote(ref, ref, self.send.at[g, e], self.recv.at[g, e], self.p.dev(dy, dz))

    def chip_copy(self, core, g, e):
        p = self.p
        one = lambda v: pl.ds(v, 1)
        if core == 0:
            zs = [p.z, p.zz(-1), p.zz(1), p.zz(-2), p.zz(2), p.zz(-3), p.zz(3), p.zz(4)][e]
            ref = self.part(g, core, pl.ds(0, NY), one(zs))
        else:
            ys = [p.y, p.yy(-1), p.yy(1), p.yy(2)][e]
            ref = self.part(g, core, one(ys), pl.ds(0, NZ))
        return remote(ref, ref, self.csend.at[g, e], self.crecv.at[g, e], p.dev(flip=True))

    ROUNDS = 7

    def round_of(self, core, g, k):
        def start(*events):
            for e in events:
                self.copy(core, g, e).start()

        def wait(*events):
            for e in events:
                self.copy(core, g, e, receive=True).wait_recv()

        def chip(*events):
            for e in events:
                self.chip_copy(core, g, e).start()

        if core == 0:
            if k == 0:
                start(0, 1)
            elif k == 1:
                wait(0, 1); start(2)
            elif k == 2:
                wait(2); start(3, 4); chip(0)
            elif k == 3:
                wait(3, 4); start(5, 6); chip(1, 2)
            elif k == 4:
                wait(5, 6); start(7, 8); chip(3, 4)
            elif k == 5:
                wait(7, 8); start(9, 10); chip(5, 6)
            else:
                wait(9, 10); chip(7)
        else:
            if k == 0:
                start(0, 1)
            elif k == 1:
                wait(0, 1); start(2, 3)
            elif k == 2:
                wait(2, 3); start(4, 5)
            elif k == 3:
                wait(4, 5); start(6)
            elif k == 4:
                wait(6); start(7, 8); chip(0)
            elif k == 5:
                wait(7, 8); start(9, 10); chip(1, 2)
            else:
                wait(9, 10); chip(3)

    def tick(self, rounds):
        for core in (0, 1):
            @pl.when(self.p.c == core)
            def _():
                for g, k in rounds:
                    self.round_of(core, g, k)

    def finish(self, g):
        for core in (0, 1):
            @pl.when(self.p.c == core)
            def _():
                for e in range(4 if core == 0 else 8):
                    self.chip_copy(1 - core, g, e).wait_recv()

    def drain(self):
        for core in (0, 1):
            @pl.when(self.p.c == core)
            def _():
                for g in range(GROUPS):
                    for e in range(EVENTS):
                        self.copy(core, g, e).wait_send()
                    for e in range(8 if core == 0 else 4):
                        self.chip_copy(core, g, e).wait_send()
        for part in (0, 1):
            self.pair_copy(part).wait_send()


GATHER_SEMS = [
    pltpu.SemaphoreType.DMA((GROUPS, EVENTS)), pltpu.SemaphoreType.DMA((GROUPS, EVENTS)),
    pltpu.SemaphoreType.DMA((GROUPS, CHIP_EVENTS)), pltpu.SemaphoreType.DMA((GROUPS, CHIP_EVENTS)),
    pltpu.SemaphoreType.DMA((2,)), pltpu.SemaphoreType.DMA((2,)),
]


def greet(devices):
    barrier = pltpu.get_barrier_semaphore()
    for device in devices:
        pl.semaphore_signal(barrier, inc=1, device_id=device, device_id_type=MESH)
    pl.semaphore_wait(barrier, len(devices))


class Reduce:
    def __init__(self, place, parts, relay, got, send, recv):
        self.p, self.parts, self.relay, self.got = place, parts, relay, got
        self.s, self.r = send, recv
        self.d = 1 - 2 * place.c

    def copies(self):
        p, d = self.p, self.d
        a = remote(self.parts.at[p.xx(2)], self.relay, self.s.at[0], self.r.at[0], p.along_x(d))
        b = remote(self.parts.at[p.xx(1)], self.got.at[0], self.s.at[1], self.r.at[1], p.along_x(1))
        c = remote(self.parts.at[p.xx(-1)], self.got.at[1], self.s.at[2], self.r.at[2], p.along_x(-1))
        e = remote(self.relay, self.got.at[2], self.s.at[3], self.r.at[3], p.along_x(d))
        return a, b, c, e

    def begin(self):
        a, b, c, _ = self.copies()
        a.start(); b.start(); c.start()

    def middle(self):
        a, _, _, e = self.copies()
        a.wait_recv(); e.start()

    def end(self):
        _, b, c, e = self.copies()
        b.wait_recv(); c.wait_recv(); e.wait_recv()

    def drain(self):
        for copy in self.copies():
            copy.wait_send()

    def total(self):
        f = jnp.float32
        return ((self.parts[self.p.x].astype(f) + self.got[0].astype(f))
                + (self.got[1].astype(f) + self.got[2].astype(f)))


class Spread:
    def __init__(self, place, full, send, recv):
        self.p, self.full, self.s, self.r = place, full, send, recv
        self.d = 1 - 2 * place.c

    def copies(self, receive=False):
        p, d = self.p, self.d
        at = self.full.at
        return (
            remote(at[p.xx(-1) if receive else p.x], at[p.xx(-1) if receive else p.x], self.s.at[0], self.r.at[0], p.along_x(1)),
            remote(at[p.xx(1) if receive else p.x], at[p.xx(1) if receive else p.x], self.s.at[1], self.r.at[1], p.along_x(-1)),
            remote(at[p.xx(2) if receive else p.xx(-d)], at[p.xx(2) if receive else p.xx(-d)], self.s.at[2], self.r.at[2], p.along_x(d)),
        )

    def begin(self):
        a, b, _ = self.copies()
        a.start(); b.start()

    def middle(self):
        a, b, _ = self.copies(receive=True)
        a.wait_recv(); b.wait_recv()
        self.copies()[2].start()

    def end(self):
        self.copies(receive=True)[2].wait_recv()

    def drain(self):
        for copy in self.copies():
            copy.wait_send()


def gather_kernel(own, out, w, pair, sem, *sems):
    p = Place()
    greet([p.dev(flip=True), p.dev(y=1), p.dev(y=-1), p.dev(z=1), p.dev(z=-1)])
    gather = Gather(p, w, own, pair, sems)
    gather.pair_copy(0).start()
    gather.pair_copy(1).start()
    gather.pair_copy(0).wait_recv()
    gather.assemble(0)
    gather.tick([(0, 0)])
    gather.pair_copy(1).wait_recv()
    for g in range(1, GROUPS):
        gather.assemble(g)
    stride = 1
    for t in range(1, stride * (GROUPS - 1) + 7):
        gather.tick([(g, t - stride * g) for g in range(GROUPS) if 0 <= t - stride * g < 7])
    for g in range(GROUPS):
        gather.finish(g)
        pltpu.make_async_copy(w.at[g], out.at[g], sem.at[g]).start()
    gather.drain()
    for g in range(GROUPS):
        pltpu.make_async_copy(w.at[g], out.at[g], sem.at[g]).wait()


def gather_weights(own):
    return pl.pallas_call(
        gather_kernel,
        out_shape=jax.ShapeDtypeStruct((GROUPS, NY, NZ, 2 * SHARD, D), jnp.bfloat16),
        in_specs=[pl.BlockSpec(memory_space=pltpu.VMEM)],
        out_specs=pl.BlockSpec(memory_space=pl.ANY),
        scratch_shapes=[
            pltpu.VMEM((GROUPS, NY, NZ, 2 * SHARD, D), jnp.bfloat16),
            pltpu.VMEM((GROUPS, SHARD, HALF), jnp.bfloat16),
            pltpu.SemaphoreType.DMA((GROUPS,)),
        ] + GATHER_SEMS,
        compiler_params=pltpu.CompilerParams(
            collective_id=0, has_side_effects=True, vmem_limit_bytes=50 << 20
        ),
        name="gather_weights",
    )(own)


HEAD_DIM = 80
GRID = 16


EPS = 1e-06


def normalize(stream):
    values_f = stream.astype(jnp.float32)
    center = values_f - jnp.mean(values_f, axis=-1, keepdims=True)
    spread = jnp.mean(center * center, axis=-1, keepdims=True)
    return (center * lax.rsqrt(spread + EPS)).astype(jnp.bfloat16)


def tensor_total(partial_value):
    return lax.psum(partial_value.astype(jnp.bfloat16), "tp").astype(jnp.float32)


def attention(normed, w_qkv, w_out_t, allowed, sample_count):
    total_rows = normed.shape[0]
    length = total_rows // sample_count
    projected = jnp.dot(normed, w_qkv, preferred_element_type=jnp.float32).astype(jnp.bfloat16)
    projected = projected.reshape(sample_count, length, -1, 3, HEAD_DIM)
    queries = projected[:, :, :, 0]
    key_part = projected[:, :, :, 1]
    value_part = projected[:, :, :, 2]
    scores = jnp.einsum(
        "bqhd,bkhd->bhqk", queries, key_part, preferred_element_type=jnp.float32
    ) * HEAD_DIM ** (-0.5)
    scores = jnp.where(allowed, scores, -1e30)
    highest = jnp.max(scores, axis=-1, keepdims=True)
    exponent = jnp.exp(scores - highest)
    weights_soft = (exponent / jnp.sum(exponent, axis=-1, keepdims=True)).astype(jnp.bfloat16)
    heads_out = jnp.einsum(
        "bhqk,bkhd->bqhd", weights_soft, value_part, preferred_element_type=jnp.float32
    )
    heads_out = heads_out.astype(jnp.bfloat16).reshape(total_rows, -1)
    return lax.dot_general(
        heads_out, w_out_t, (((1,), (1,)), ((), ())), preferred_element_type=jnp.float32
    )


def feed_forward(normed, w_up, w_down_t):
    hidden = jax.nn.gelu(
        jnp.dot(normed, w_up, preferred_element_type=jnp.float32), approximate=False
    )
    hidden = hidden.astype(jnp.bfloat16)
    return lax.dot_general(
        hidden, w_down_t, (((1,), (1,)), ((), ())), preferred_element_type=jnp.float32
    )


def transformer_layer(stream, weights, allowed, sample_count):
    w_qkv, w_out_t, w_up, w_down_t = weights
    attended = attention(normalize(stream), w_qkv, w_out_t, allowed, sample_count)
    middle = (stream.astype(jnp.float32) + tensor_total(attended)).astype(jnp.bfloat16)
    result_rows = middle.astype(jnp.float32) + tensor_total(
        feed_forward(normalize(middle), w_up, w_down_t)
    )
    result_rows = result_rows.astype(jnp.bfloat16)
    return result_rows


def on_device(
    patches,
    half_grid,
    text_embed,
    dest_dev,
    dest_pos,
    text_len,
    enc_qkv,
    enc_out_t,
    enc_up,
    enc_down_t,
    merge_t,
    dec_qkv,
    dec_out_t,
    dec_up,
    dec_down_t,
):
    image_count = half_grid.shape[0]
    model_width = patches.shape[1]
    per_image = GRID * GRID
    patch_index = jnp.arange(per_image, dtype=jnp.int32)
    key_valid = ((patch_index // GRID)[None, :] < 2 * half_grid[:, 0:1]) & (
        (patch_index % GRID)[None, :] < 2 * half_grid[:, 1:2]
    )
    own = jnp.concatenate(
        [enc_qkv, enc_out_t, enc_up, enc_down_t, merge_t, dec_qkv, dec_out_t, dec_up, dec_down_t], axis=1
    )
    own = own.reshape(SHARD, GROUPS, 2, HALF).transpose(2, 1, 0, 3)
    w = gather_weights(own).reshape(GROUPS, D, D)
    enc_weights = (w[0, :, :960], w[0, :, 960:], w[1], w[2])
    merge_local = w[3]
    qkv_dec, out_dec, up_dec, down_dec = w[4, :, :960], w[4, :, 960:], w[5], w[6]
    encoded = transformer_layer(patches, enc_weights, key_valid[:, None, None, :], image_count)
    half_side = GRID // 2
    blocks = encoded.reshape(image_count, half_side, 2, half_side, 2, model_width).transpose(
        0, 1, 3, 2, 4, 5
    )
    blocks = blocks.reshape(image_count * half_side * half_side, 4 * model_width)
    span_width = merge_local.shape[1]
    feature_part = lax.dynamic_slice_in_dim(
        blocks, lax.axis_index("tp") * span_width, span_width, 1
    )
    merge_partial = lax.dot_general(
        feature_part, merge_local, (((1,), (1,)), ((), ())), preferred_element_type=jnp.float32
    )
    merged = tensor_total(merge_partial).astype(jnp.bfloat16)
    slot_count = merged.shape[0]
    senders = lax.axis_size("req")
    even_share = slot_count // senders
    capacity = even_share + max(even_share // 2, 1)
    cell_index = jnp.arange(half_side * half_side, dtype=jnp.int32)
    slot_valid = ((cell_index // half_side)[None, :] < half_grid[:, 0:1]) & (
        (cell_index % half_side)[None, :] < half_grid[:, 1:2]
    )
    slot_valid = slot_valid.reshape(slot_count)
    one_hot = (dest_dev[:, None] == jnp.arange(senders, dtype=jnp.int32)[None, :]).astype(jnp.int32)
    earlier = jnp.cumsum(one_hot, axis=0) - one_hot
    slot_rank = jnp.sum(earlier * one_hot, axis=1)
    outgoing = (
        jnp.zeros((senders, capacity, model_width), jnp.bfloat16)
        .at[dest_dev, slot_rank]
        .set(merged)
    )
    out_pos = (
        jnp.full((senders, capacity), -1, jnp.int32)
        .at[dest_dev, slot_rank]
        .set(jnp.where(slot_valid, dest_pos, -1))
    )
    incoming, in_pos = (
        lax.all_to_all(outgoing, "req", split_axis=0, concat_axis=0, tiled=True),
        lax.all_to_all(out_pos, "req", split_axis=0, concat_axis=0, tiled=True),
    )
    seq_len = text_embed.shape[0]
    target = jnp.where(in_pos >= 0, in_pos, seq_len).astype(jnp.int32).reshape(-1)
    dec_input = text_embed.at[target].set(incoming.reshape(-1, model_width), mode="drop")
    positions = jnp.arange(seq_len, dtype=jnp.int32)
    causal = (positions[:, None] >= positions[None, :])[None, None]
    decoded = transformer_layer(dec_input, (qkv_dec, out_dec, up_dec, down_dec), causal, 1)
    keep_mask = positions < slot_count + text_len[0]
    return jnp.where(keep_mask[:, None], decoded, jnp.zeros_like(decoded))


def solution(mesh):
    return jax.shard_map(
        on_device,
        mesh=mesh,
        in_specs=(
            P("req", None),
            P("req", None),
            P("req", None),
            P("req"),
            P("req"),
            P("req"),
            P("req", "tp"),
            P("req", "tp"),
            P("req", "tp"),
            P("req", "tp"),
            P("req", "tp"),
            P("req", "tp"),
            P("req", "tp"),
            P("req", "tp"),
            P("req", "tp"),
        ),
        out_specs=P("req", None),
        check_vma=False,
    )
```
